128 devices in a mesh: chan: 8 (over y, core), facet: 16 (over z, x).
Axes of the slice: x: 4, y: 4, z: 4, core: 2. Of those that a mesh axis runs over, the one named last changes fastest.
Arguments:
- visibilities: bfloat16 [32, 8, 8, 65536], P(None, None, 'chan', 'facet'), may hold values from -6 to 6
- w_kernel: bfloat16 [32, 2, 8], replicated, may hold values from -2 to 2
- w_index: int32 [8, 65536], P(None, 'facet'), may hold values from 0 to 31
- cell_offsets: int32 [2, 8, 65536], P(None, None, 'facet'), may hold values from 0 to 24
- block_sub: int32 [8, 128], P(None, 'facet'), may hold values from 0 to 31
- intersection_rows: int32 [16, 32], replicated, may hold values from 0 to 63, as said below
- intersection_count: int32 [16], replicated, may hold values from 1 to 32, as said below
Outputs:
- sky_image: float32 [32, 4, 64, 32768], P('chan', None, None, 'facet')
The draws below stay inside these ranges and needn't reach their ends.
Inputs may be any that keep to these rules, and one draw needn't show every extreme that they name: `intersection_rows`: the rows in one facet's list are distinct. `intersection_count`: some facet other than the last has exactly 32 entries in use.
All inputs are finite; a program needn't handle non-finite values.
Results may differ from the reference program's by a relative error of at most 0.0059.
Values may be sent and summed in bfloat16 or wider, within the bound.
A program may use at most 128 MiB of HBM per device.

```python
import math
import jax
import jax.numpy as jnp
import numpy as np
from jax import lax

POL = 4
ROWS_DEV = 4096
BLK = 512
SG = 32
KS = 8
W = 32
NSUB = 32
FX = 2048
FY = 64
MARGIN = 128
MAXS = 32
GROUPS = 8
FACETS = 16
CHANS = 32
ROWS = 65536
BLOCKS = 128
NX = 32768


def draw_intersection_rows(key, part):
    facet_keys = jax.random.split(key, FACETS)

    def one_facet(sub_key):
        return jax.random.permutation(sub_key, FY)[:MAXS]
    return jax.vmap(one_facet)(facet_keys).astype(jnp.int32)


def draw_intersection_count(key, part):
    count_key, full_key = jax.random.split(jax.random.fold_in(key, 7))
    counts = jax.random.randint(count_key, (FACETS,), 1, MAXS + 1)
    full_facet = jax.random.randint(full_key, (), 0, FACETS - 1)
    return jnp.where(jnp.arange(FACETS) == full_facet, MAXS, counts).astype(jnp.int32)


def touch_ends(array, own_key, smallest, largest):
    shape = array.shape
    spot = [jax.random.randint(jax.random.fold_in(own_key, axis), (), 0, shape[axis]) for axis in range(len(shape))]
    array = array.at[tuple(spot)].set(smallest)
    longest = shape.index(max(shape))
    spot[longest] = (spot[longest] + 1) % shape[longest]
    return array.at[tuple(spot)].set(largest)


def level_of(stream_key, shape, cuts, low, top_value):
    factor_of = 1.0
    for dim, shards_of in cuts:
        draws = jax.random.uniform(jax.random.fold_in(jax.random.fold_in(stream_key, 6), dim), (shards_of,), jnp.float32, low / len(cuts), top_value / len(cuts))
        factor_of = factor_of * jnp.repeat(jnp.exp(draws), shape[dim] // shards_of).reshape((-1,) + (1,) * (len(shape) - 1 - dim))
    return factor_of


def rank_table(amount, slope):
    loads = [(1 << 20) // math.isqrt(grade ** slope) + 1 for grade in range(1, amount + 1)]
    scale = 1 + sum(loads) // (1 << 30)
    return np.cumsum(np.array([max(1, weight // scale) for weight in loads]))


def ranked_ids(rng, extent, number_of, slope):
    listing = rank_table(number_of, slope)
    pick = jax.random.randint(jax.random.fold_in(rng, 1), extent, 0, int(listing[number_of - 1]))
    standing = jnp.searchsorted(jnp.asarray(listing, jnp.int32), pick, side="right")
    return jax.random.permutation(jax.random.fold_in(rng, 2), number_of)[standing].astype(jnp.int32)


def noise(rng, shape, deviation, bound, cuts=(), kind=jnp.bfloat16):
    factor_of = level_of(rng, shape, cuts, -0.22, 0.18) if cuts else 1.0
    array = jax.random.normal(rng, shape, jnp.float32) * deviation * factor_of
    return jnp.minimum(jnp.maximum(array, -bound), bound).astype(kind)


def setup_inputs(seed: int = 0) -> dict:
    splits = jax.random.split(jax.random.key(seed), 8)
    return {
        "visibilities": noise(splits[0], (CHANS, 2 * POL, GROUPS, ROWS), 1.0, 6.0, ((2, 8), (3, 16))),
        "w_kernel": noise(splits[1], (W, 2, KS), KS ** -0.5, 2.0),
        "w_index": touch_ends(jax.random.randint(splits[2], (GROUPS, ROWS), 0, W), jax.random.fold_in(splits[2], 1), 0, W - 1).astype(jnp.int32),
        "cell_offsets": touch_ends(jax.random.randint(splits[3], (2, GROUPS, ROWS), 0, SG - KS + 1), jax.random.fold_in(splits[3], 1), 0, SG - KS).astype(jnp.int32),
        "block_sub": touch_ends(ranked_ids(splits[4], (GROUPS, BLOCKS), NSUB, 2), jax.random.fold_in(splits[4], 3), 0, NSUB - 1).astype(jnp.int32),
        "intersection_rows": draw_intersection_rows(jax.random.fold_in(splits[7], 71), 0),
        "intersection_count": draw_intersection_count(jax.random.fold_in(splits[7], 71), 0),
    }


def anchors(sub_index, side_len, period):
    span = period // side_len
    row_anchor = (jnp.mod(sub_index * 37, span) - span // 2) * side_len
    col_anchor = (jnp.mod(sub_index * 53 + 5, span) - span // 2) * side_len
    return (row_anchor, col_anchor)

def row_tables(sub_index, side_len, height, period):
    row_anchor, col_anchor = anchors(sub_index, side_len, period)
    cell_ids = jnp.arange(side_len, dtype=jnp.int32)
    line_ids = jnp.arange(height, dtype=jnp.int32) - height // 2
    phase_int = (row_anchor[:, None, None] + cell_ids[None, None, :]) * line_ids[None, :, None]
    radians = jnp.mod(phase_int, period).astype(jnp.float32) * (2.0 * math.pi / period)
    return (jnp.cos(radians).astype(jnp.bfloat16), jnp.sin(radians).astype(jnp.bfloat16))

def col_tables(sub_index, side_len, col_ids, period):
    row_anchor, col_anchor = anchors(sub_index, side_len, period)
    cell_ids = jnp.arange(side_len, dtype=jnp.int32)
    phase_int = (col_anchor[:, None, None] + cell_ids[None, :, None]) * (col_ids - period // 2)[None, None, :]
    radians = jnp.mod(phase_int, period).astype(jnp.float32) * (2.0 * math.pi / period)
    return (jnp.cos(radians).astype(jnp.bfloat16), (-jnp.sin(radians)).astype(jnp.bfloat16))

def place_kernel(values, offsets, side_len):
    distance = jnp.arange(side_len, dtype=jnp.int32)[:, None] - offsets[None, :]
    running = jnp.zeros((values.shape[0], side_len, offsets.shape[0]), jnp.float32)
    for tap_idx in range(values.shape[1]):
        running = running + values[:, tap_idx, None, :] * (distance == tap_idx).astype(jnp.float32)[None]
    return running

def combine(products, side_len, row_width):
    real_part = products[:, :side_len, :row_width] - products[:, side_len:, row_width:]
    imag_part = products[:, :side_len, row_width:] + products[:, side_len:, :row_width]
    return jnp.stack([real_part, imag_part], axis=1)

def block_terms(vis_part, plane_ids, cell_pos, kernel, side_len, block_len):
    planes = kernel.shape[0]
    plane_pick = (jnp.arange(planes, dtype=jnp.int32)[:, None] == plane_ids[None, :]).astype(jnp.float32)
    values = jnp.einsum('wqk,wr->qkr', kernel.astype(jnp.float32), plane_pick, precision=lax.Precision.HIGHEST)
    left_kern = place_kernel(values, cell_pos[0], side_len).astype(jnp.bfloat16)
    right_kern = place_kernel(values, cell_pos[1], side_len)
    num_pols = vis_part.shape[1] // 2
    vis_real = vis_part[:, :num_pols].astype(jnp.float32)[:, :, None, :]
    vis_imag = vis_part[:, num_pols:].astype(jnp.float32)[:, :, None, :]
    y_real = (vis_real * right_kern[0][None, None] - vis_imag * right_kern[1][None, None]).astype(jnp.bfloat16)
    y_imag = (vis_real * right_kern[1][None, None] + vis_imag * right_kern[0][None, None]).astype(jnp.bfloat16)
    num_rows = plane_ids.shape[0]
    blocks = num_rows // block_len
    row_width = vis_part.shape[0] * num_pols * side_len
    stacked = jnp.concatenate([y_real.reshape(row_width, blocks, block_len), y_imag.reshape(row_width, blocks, block_len)], axis=0)
    left_flat = left_kern.reshape(2 * side_len, blocks, block_len)
    products = lax.dot_general(left_flat.astype(jnp.float32), stacked.astype(jnp.float32), (((2,), (2,)), ((1,), (1,))), precision=lax.Precision.HIGHEST, preferred_element_type=jnp.float32)
    return combine(products, side_len, row_width)

def to_rows(subgrid, row_cos, row_sin, img_scale):
    sub_real = subgrid[:, 0].astype(jnp.float32)
    sub_imag = subgrid[:, 1].astype(jnp.float32)
    cos_full = row_cos.astype(jnp.float32)
    sin_full = row_sin.astype(jnp.float32)

    def apply_table(table, data):
        return jnp.einsum('gyu,guq->gyq', table, data, precision=lax.Precision.HIGHEST)
    real_part = apply_table(cos_full, sub_real) - apply_table(sin_full, sub_imag)
    imag_part = apply_table(cos_full, sub_imag) + apply_table(sin_full, sub_real)
    return (jnp.stack([real_part, imag_part], axis=1) * img_scale).astype(jnp.bfloat16)

def reference(visibilities, w_kernel, w_index, cell_offsets, block_sub, intersection_rows, intersection_count):
    per_dev = ROWS_DEV // BLK
    row_width = CHANS * POL * SG

    def grid_step(running, segment):
        group_id = segment // FACETS
        row_start = segment % FACETS * ROWS_DEV
        vis_part = lax.dynamic_index_in_dim(visibilities, group_id, 2, keepdims=False)
        vis_part = lax.dynamic_slice_in_dim(vis_part, row_start, ROWS_DEV, 2)
        plane_ids = lax.dynamic_slice_in_dim(lax.dynamic_index_in_dim(w_index, group_id, 0, keepdims=False), row_start, ROWS_DEV, 0)
        cell_pos = lax.dynamic_slice_in_dim(lax.dynamic_index_in_dim(cell_offsets, group_id, 1, keepdims=False), row_start, ROWS_DEV, 1)
        sub_ids = lax.dynamic_slice_in_dim(lax.dynamic_index_in_dim(block_sub, group_id, 0, keepdims=False), row_start // BLK, per_dev, 0)
        block_sums = block_terms(vis_part, plane_ids, cell_pos, w_kernel, SG, BLK)
        plane_pick = (jnp.arange(NSUB, dtype=jnp.int32)[:, None] == sub_ids[None, :]).astype(jnp.float32)
        increment = jnp.dot(plane_pick, block_sums.reshape(per_dev, 2 * SG * row_width), precision=lax.Precision.HIGHEST)
        return (running + increment, None)
    grid_init = jnp.zeros((NSUB, 2 * SG * row_width), jnp.float32)
    running, unused = lax.scan(grid_step, grid_init, jnp.arange(GROUPS * FACETS, dtype=jnp.int32))
    subgrid = running.reshape(NSUB, 2, SG, row_width).astype(jnp.bfloat16)
    sub_index = jnp.arange(NSUB, dtype=jnp.int32)
    row_cos, row_sin = row_tables(sub_index, SG, FY, NX)
    img_scale = 1.0 / math.sqrt(GROUPS * ROWS)
    row_image = to_rows(subgrid, row_cos, row_sin, img_scale)
    row_split = row_image.reshape(NSUB, 2, FY, CHANS * POL, SG).astype(jnp.float32)

    def facet_image(facet_id):
        col_ids = facet_id * FX + jnp.arange(FX, dtype=jnp.int32)
        col_cos, col_sin = col_tables(sub_index, SG, col_ids, NX)
        col_table = jnp.stack([col_cos, col_sin], axis=1).astype(jnp.float32)
        return jnp.einsum('grycv,grvx->cyx', row_split, col_table, precision=lax.Precision.HIGHEST)
    images = lax.map(facet_image, jnp.arange(FACETS, dtype=jnp.int32))
    line_ids = jnp.arange(FY, dtype=jnp.int32)
    slot_ids = jnp.arange(MAXS, dtype=jnp.int32)
    chosen = ((intersection_rows[:, :, None] == line_ids[None, None, :]) & (slot_ids[None, :, None] < intersection_count[:, None, None])).astype(jnp.float32)
    row_keep = lax.optimization_barrier(jnp.sum(chosen, axis=1))
    sent_band = images[:, :, :, FX - MARGIN:] * row_keep[:, None, :, None]
    arrived = jnp.concatenate([jnp.zeros_like(sent_band[:1]), sent_band[:-1]], axis=0)
    sky_image = jnp.concatenate([images[:, :, :, :MARGIN] + arrived, images[:, :, :, MARGIN:]], axis=3)
    sky_image = sky_image.reshape(FACETS, CHANS, POL, FY, FX).transpose(1, 2, 3, 0, 4)
    return sky_image.reshape(CHANS, POL, FY, NX)
```

```python
import math

import jax
import jax.numpy as jnp
import numpy as np
from jax import lax
from jax.experimental import pallas as pl
from jax.experimental.pallas import tpu as pltpu
from jax.sharding import PartitionSpec as P

BLK = 512
SG = 32
NSUB = 32
FX = 2048
FY = 64
MARGIN = 128
NX = 32768
GROUPS = 8
NB = 64
CH = 4
POL = 4
STAGES = 2
CPS = CH // STAGES
NL = CPS * POL * SG
RING = 4
BF = jnp.bfloat16
F32 = jnp.float32
MESH = pl.DeviceIdType.MESH


def sort_plan(block_sub):
    sub = block_sub.reshape(NB)
    ids = jnp.arange(NB, dtype=jnp.int32)
    before = (sub[None, :] < sub[:, None]) | (
        (sub[None, :] == sub[:, None]) & (ids[None, :] < ids[:, None])
    )
    rank = jnp.sum(before.astype(jnp.int32), axis=1)
    hit = rank[None, :] == ids[:, None]
    order = jnp.sum(jnp.where(hit, ids[None, :], 0), axis=1)
    placed = jnp.sum(jnp.where(hit, sub[None, :], 0), axis=1)
    same = jnp.concatenate([jnp.zeros((1,), jnp.bool_), placed[1:] == placed[:-1]])
    want = jnp.arange(NSUB, dtype=jnp.int32)[:, None]
    last = jnp.maximum(jnp.sum((sub[None, :] <= want).astype(jnp.int32), axis=1) - 1, 0)
    has = jnp.any(sub[None, :] == want, axis=1)
    return order, same.astype(F32), last, has.astype(F32)


def gather_kernel(
    vis,
    widx_h,
    offs_h,
    table,
    order,
    same,
    last,
    has,
    grid_out,
    *scratch,
):
    recv = scratch[:STAGES]
    (
        widx,
        offs,
        left,
        right,
        pref,
        part,
        in1,
        mid,
        in2,
        local_sem,
        turn_send,
        turn_recv,
        own_sem,
        ring_send,
        ring_recv,
    ) = scratch[STAGES:]
    me = lax.axis_index("chan")
    facet = lax.axis_index("facet")
    mz = lax.div(facet, RING)
    mx = lax.rem(facet, RING)

    def x_peer(k):
        return lax.rem(mx + k, RING)

    def z_peer(k):
        return lax.rem(mz + k, RING)

    def on_x(x):
        return {"facet": mz * 4 + x}

    def on_z(z):
        return {"facet": z * 4 + mx}

    load_w = pltpu.make_async_copy(widx_h, widx, local_sem.at[0])
    load_o = pltpu.make_async_copy(offs_h, offs, local_sem.at[1])
    load_w.start()
    load_o.start()

    def block_refs(dest, source, st, blk):
        src = vis.at[pl.ds(dest * CH + st * CPS, CPS), :, pl.ds(blk * BLK, BLK)]
        return src, recv[st].at[source * 8 + blk]

    def slab(source, st):
        return recv[st].at[pl.ds(source * 8, 8)]

    for st in range(STAGES):
        for blk in range(8):
            src, dst = block_refs(me, me, st, blk)
            pltpu.make_async_copy(src, dst, own_sem.at[st]).start()

    barrier = pltpu.get_barrier_semaphore()
    for k in range(1, GROUPS):
        peer = lax.rem(me + k, GROUPS)
        pl.semaphore_signal(barrier, inc=1, device_id={"chan": peer}, device_id_type=MESH)
    for k in range(1, RING):
        pl.semaphore_signal(barrier, inc=1, device_id=on_x(x_peer(k)), device_id_type=MESH)
        pl.semaphore_signal(barrier, inc=1, device_id=on_z(z_peer(k)), device_id_type=MESH)
    pl.semaphore_wait(barrier, GROUPS - 1 + 2 * (RING - 1))

    for st in range(STAGES):
        for k in range(1, GROUPS):
            peer = lax.rem(me + k, GROUPS)
            for blk in range(8):
                src, dst = block_refs(peer, me, st, blk)
                pltpu.make_async_remote_copy(
                    src_ref=src,
                    dst_ref=dst,
                    send_sem=turn_send.at[st, k - 1],
                    recv_sem=turn_recv.at[st, k - 1],
                    device_id={"chan": peer},
                    device_id_type=MESH,
                ).start()

    def turned(st):
        mine = slab(me, st)
        pltpu.make_async_copy(mine, mine, own_sem.at[st]).wait()
        for k in range(1, GROUPS):
            peer = lax.rem(me + GROUPS - k, GROUPS)
            got = slab(peer, st)
            pltpu.make_async_remote_copy(
                src_ref=got,
                dst_ref=got,
                send_sem=turn_send.at[st, k - 1],
                recv_sem=turn_recv.at[st, k - 1],
                device_id={"chan": peer},
                device_id_type=MESH,
            ).wait()

    load_w.wait()
    load_o.wait()

    iota8 = lax.broadcasted_iota(jnp.int32, (8, 128), 0)
    tab_re = table[0]
    tab_im = table[1]

    def prep(tile, carry):
        lanes = pl.ds(pl.multiple_of(tile * 128, 128), 128)
        blk = lax.div(tile, 4)
        col = lax.rem(tile, 4) * 128
        cols = pl.ds(pl.multiple_of(col, 128), 128)
        cols_im = pl.ds(pl.multiple_of(col + BLK, 128), 128)
        planes = widx[:, lanes]
        offset = (offs[0, :, lanes], offs[1, :, lanes])
        for g in range(GROUPS):
            b = g * 8 + blk
            plane = jnp.broadcast_to(planes[g : g + 1], (8, 128))
            val_re = jnp.take_along_axis(tab_re, plane, axis=1)
            val_im = jnp.take_along_axis(tab_im, plane, axis=1)
            for side in range(2):
                off = jnp.broadcast_to(offset[side][g : g + 1], (8, 128))
                dist = iota8 - off
                cyc = lax.bitwise_and(dist, 7)
                tap_re = jnp.take_along_axis(val_re, cyc, axis=0)
                tap_im = jnp.take_along_axis(val_im, cyc, axis=0)
                res, ims = [], []
                for q in range(SG // 8):
                    ok = lax.bitwise_and(dist + 8 * q, -8) == 0
                    res.append(jnp.where(ok, tap_re, 0.0))
                    ims.append(jnp.where(ok, tap_im, 0.0))
                k_re = jnp.concatenate(res, axis=0)
                k_im = jnp.concatenate(ims, axis=0)
                if side == 0:
                    re16 = k_re.astype(BF)
                    left[b, 0:SG, cols] = re16
                    left[b, 0:SG, cols_im] = (-k_im).astype(BF)
                    left[b, SG : 2 * SG, cols] = k_im.astype(BF)
                    left[b, SG : 2 * SG, cols_im] = re16
                else:
                    right[b, 0, :, cols] = k_re
                    right[b, 1, :, cols] = k_im
        return carry

    lax.fori_loop(0, GROUPS * BLK // 128, prep, 0)

    def grid_part(st, lo, hi, run):
        def body(j, run):
            b = order[j]
            kern = right[b]
            k_re = kern[0]
            k_im = kern[1]
            seen = recv[st][b]
            rows = []
            for c in range(CPS):
                v = seen[c].astype(F32)
                for p in range(POL):
                    v_re = jnp.broadcast_to(v[p : p + 1], (SG, BLK))
                    v_im = jnp.broadcast_to(v[p + POL : p + POL + 1], (SG, BLK))
                    y_re = (v_re * k_re - v_im * k_im).astype(BF)
                    y_im = (v_re * k_im + v_im * k_re).astype(BF)
                    rows.append(jnp.concatenate([y_re, y_im], axis=1))
            y = jnp.concatenate(rows, axis=0)
            o = lax.dot_general(
                left[b], y, (((1,), (1,)), ((), ())), preferred_element_type=F32
            )
            run = run * same[j] + o
            pref[j] = run
            return run

        return lax.fori_loop(lo, hi, body, run, unroll=4)

    def emit(st):
        def body(s, carry):
            part[st, s] = (pref[last[s]] * has[s]).astype(BF)
            return carry

        lax.fori_loop(0, NSUB, body, 0)

    def ring_copy(st, half, phase, k, src, dst, dev):
        return pltpu.make_async_remote_copy(
            src_ref=src,
            dst_ref=dst,
            send_sem=ring_send.at[st, half, phase, k - 1],
            recv_sem=ring_recv.at[st, half, phase, k - 1],
            device_id=dev,
            device_id_type=MESH,
        )

    copies = {}
    half_n = NSUB // 2
    first = (mx, mz)
    second = (mz, mx)

    def dev_of(half, phase_axis, k):
        along_x = (half == 0) == (phase_axis == 0)
        return (x_peer(k), on_x(x_peer(k))) if along_x else (z_peer(k), on_z(z_peer(k)))

    def rs1(st):
        for half in range(2):
            for k in range(1, RING):
                pos, dev = dev_of(half, 0, k)
                cp = ring_copy(
                    st,
                    half,
                    0,
                    k,
                    part.at[st, pl.ds(half * half_n + 4 * pos, 4)],
                    in1.at[st, half, k - 1],
                    dev,
                )
                cp.start()
                copies[st, half, 0, k] = cp

    def rs2(st):
        for half in range(2):
            for k in range(1, RING):
                copies[st, half, 0, k].wait()
            total = part[st, pl.ds(half * half_n + 4 * first[half], 4)].astype(F32)
            for k in range(1, RING):
                total = total + in1[st, half, k - 1].astype(F32)
            mid[st, half] = total.astype(BF)
            for k in range(1, RING):
                pos, dev = dev_of(half, 1, k)
                cp = ring_copy(st, half, 1, k, mid.at[st, half, pos], in2.at[st, half, k - 1], dev)
                cp.start()
                copies[st, half, 1, k] = cp

    def ag1(st):
        for half in range(2):
            for k in range(1, RING):
                copies[st, half, 1, k].wait()
            total = mid[st, half, second[half]].astype(F32)
            for k in range(1, RING):
                total = total + in2[st, half, k - 1].astype(F32)
            slot = half * half_n + 4 * first[half] + second[half]
            grid_out[st, slot] = total.astype(BF)
            for k in range(1, RING):
                pos, dev = dev_of(half, 1, k)
                cp = ring_copy(
                    st, half, 2, k, grid_out.at[st, slot], grid_out.at[st, slot], dev
                )
                cp.start()
                copies[st, half, 2, k] = cp

    def ag2(st):
        for half in range(2):
            for k in range(1, RING):
                copies[st, half, 2, k].wait()
            span = pl.ds(half * half_n + 4 * first[half], 4)
            for k in range(1, RING):
                pos, dev = dev_of(half, 0, k)
                cp = ring_copy(
                    st, half, 3, k, grid_out.at[st, span], grid_out.at[st, span], dev
                )
                cp.start()
                copies[st, half, 3, k] = cp

    def finish(st):
        for half in range(2):
            for k in range(1, RING):
                copies[st, half, 3, k].wait()

    steps = []
    for st in range(STAGES):
        turned(st)
        run = jnp.zeros((2 * SG, NL), F32)
        for piece in range(4):
            run = grid_part(st, piece * (NB // 4), (piece + 1) * (NB // 4), run)
            if steps:
                steps.pop(0)()
        emit(st)
        rs1(st)
        steps += [
            (lambda st=st: rs2(st)),
            (lambda st=st: ag1(st)),
            (lambda st=st: ag2(st)),
            (lambda st=st: finish(st)),
        ]
    for step in steps:
        step()


def gridded(vis, w_index, offsets, table, plan):
    any_spec = pl.BlockSpec(memory_space=pl.ANY)
    vmem = pl.BlockSpec(memory_space=pltpu.VMEM)
    smem = pl.BlockSpec(memory_space=pltpu.SMEM)
    return pl.pallas_call(
        gather_kernel,
        out_shape=jax.ShapeDtypeStruct((STAGES, NSUB, 2 * SG, NL), BF),
        in_specs=[any_spec, any_spec, any_spec, vmem, smem, smem, smem, smem],
        out_specs=vmem,
        scratch_shapes=[
            *[pltpu.VMEM((NB, CPS, 2 * POL, BLK), BF)] * STAGES,
            pltpu.VMEM((GROUPS, GROUPS * BLK), jnp.int32),
            pltpu.VMEM((2, GROUPS, GROUPS * BLK), jnp.int32),
            pltpu.VMEM((NB, 2 * SG, 2 * BLK), BF),
            pltpu.VMEM((NB, 2, SG, BLK), F32),
            pltpu.VMEM((NB, 2 * SG, NL), F32),
            pltpu.VMEM((STAGES, NSUB, 2 * SG, NL), BF),
            pltpu.VMEM((STAGES, 2, RING - 1, 4, 2 * SG, NL), BF),
            pltpu.VMEM((STAGES, 2, 4, 2 * SG, NL), BF),
            pltpu.VMEM((STAGES, 2, RING - 1, 2 * SG, NL), BF),
            pltpu.SemaphoreType.DMA((2,)),
            pltpu.SemaphoreType.DMA((STAGES, GROUPS - 1)),
            pltpu.SemaphoreType.DMA((STAGES, GROUPS - 1)),
            pltpu.SemaphoreType.DMA((STAGES,)),
            pltpu.SemaphoreType.DMA((STAGES, 2, 4, RING - 1)),
            pltpu.SemaphoreType.DMA((STAGES, 2, 4, RING - 1)),
        ],
        compiler_params=pltpu.CompilerParams(
            collective_id=0, has_side_effects=True, vmem_limit_bytes=60 * 2**20
        ),
        name="turn_grid_share",
    )(vis, w_index, offsets, table, *plan)


XT = 256
NT = FX // XT


def image_kernel(grids, row_tab, e_cos, e_sin, w_cos, w_sin, keep, out, z, col, edge, cur):
    step = pl.program_id(0)
    kblk = 128

    def rotate(q):
        rows = pl.ds(q * kblk, kblk)
        c = cur[0, rows]
        s = cur[1, rows]
        wc = w_cos[rows]
        ws = w_sin[rows]
        cur[0, rows] = c * wc - s * ws
        cur[1, rows] = s * wc + c * ws
        return c, s

    def fill(width):
        for q in range(NSUB * SG // kblk):
            for h in range(width // 128):
                c, s = rotate(q)
                col[pl.ds(q * 2 * kblk, kblk), pl.ds(h * 128, 128)] = c.astype(BF)
                col[pl.ds(q * 2 * kblk + kblk, kblk), pl.ds(h * 128, 128)] = (-s).astype(BF)

    @pl.when(step == 0)
    def _():
        img_scale = 1.0 / math.sqrt(GROUPS * 65536)

        def rows4(q, carry):
            for st in range(STAGES):
                os = []
                for gi in range(4):
                    g = q * 4 + gi
                    os.append(
                        jnp.dot(row_tab[g], grids[st, g], preferred_element_type=F32) * img_scale
                    )
                for c in range(CPS):
                    for p in range(POL):
                        lo = c * POL * SG + p * SG
                        both = jnp.concatenate([o[:, lo : lo + SG] for o in os], axis=1).astype(BF)
                        base = (st * CPS + c) * POL * FY + p * FY
                        lanes0 = pl.ds(pl.multiple_of(q * 256, 128), 128)
                        lanes1 = pl.ds(pl.multiple_of(q * 256 + 128, 128), 128)
                        z[pl.ds(base, FY), lanes0] = both[:FY]
                        z[pl.ds(base, FY), lanes1] = both[FY:]
            return carry

        lax.fori_loop(0, NSUB // 4, rows4, 0)
        cur[0] = e_cos[...]
        cur[1] = e_sin[...]
        fill(128)
        prev = jnp.dot(z[...], col[:, 0:128], preferred_element_type=F32)
        edge[...] = prev * keep[...]

    fill(XT)
    o = jnp.dot(z[...], col[...], preferred_element_type=F32)
    out[...] = o.reshape(CH, POL, FY, XT)

    @pl.when(step == 0)
    def _():
        out[:, :, :, 0:MARGIN] = out[:, :, :, 0:MARGIN] + edge[...].reshape(CH, POL, FY, MARGIN)


def imaged(grids, row_tab, e_cos, e_sin, w_cos, w_sin, keep):
    def whole(shape):
        return pl.BlockSpec(shape, lambda n: (0,) * len(shape), pipeline_mode=pl.Buffered(1))

    return pl.pallas_call(
        image_kernel,
        grid=(NT,),
        out_shape=jax.ShapeDtypeStruct((CH, POL, FY, FX), F32),
        in_specs=[
            whole(a.shape) for a in (grids, row_tab, e_cos, e_sin, w_cos, w_sin, keep)
        ],
        out_specs=pl.BlockSpec((CH, POL, FY, XT), lambda n: (0, 0, 0, n)),
        scratch_shapes=[
            pltpu.VMEM((CH * POL * FY, NSUB * SG * 2), BF),
            pltpu.VMEM((NSUB * SG * 2, XT), BF),
            pltpu.VMEM((CH * POL * FY, MARGIN), F32),
            pltpu.VMEM((2, NSUB * SG, 128), F32),
        ],
        compiler_params=pltpu.CompilerParams(vmem_limit_bytes=60 * 2**20),
        name="facet_image",
    )(grids, row_tab, e_cos, e_sin, w_cos, w_sin, keep)


def row_table():
    g = np.arange(NSUB)
    span = NX // SG
    anchor = ((37 * g) % span - span // 2) * SG
    lines = np.arange(FY) - FY // 2
    phase = ((anchor[:, None, None] + np.arange(SG)[None, None, :]) * lines[None, :, None]) % NX
    rad = phase.astype(np.float32) * np.float32(2.0 * math.pi / NX)
    cos, sin = np.cos(rad), np.sin(rad)
    top = np.concatenate([cos, -sin], axis=2)
    low = np.concatenate([sin, cos], axis=2)
    return np.concatenate([top, low], axis=1)


def shards(
    visibilities, w_kernel, w_index, cell_offsets, block_sub, intersection_rows, intersection_count
):
    facet = lax.axis_index("facet")
    vis = visibilities.reshape(visibilities.shape[0], 2 * POL, w_index.shape[1])
    table = jnp.pad(
        w_kernel.astype(F32).transpose(1, 2, 0), ((0, 0), (0, 0), (0, 128 - w_kernel.shape[0]))
    )
    grids = gridded(vis, w_index, cell_offsets, table, sort_plan(block_sub))

    g = np.arange(NSUB)
    span = NX // SG
    anchor = ((53 * g + 5) % span - span // 2) * SG
    freq = jnp.asarray((anchor[:, None] + np.arange(SG)[None, :]).reshape(-1, 1), jnp.int32)
    start = facet * FX - NX // 2 - MARGIN
    cols = start + jnp.arange(128, dtype=jnp.int32)[None, :]
    to_rad = 2.0 * math.pi / NX
    rad = jnp.mod(freq * cols, NX).astype(F32) * to_rad
    turn = jnp.broadcast_to(jnp.mod(freq * 128, NX).astype(F32) * to_rad, rad.shape)

    before = jnp.maximum(facet - 1, 0)
    listed = lax.dynamic_index_in_dim(intersection_rows, before, 0, keepdims=False)
    in_use = lax.dynamic_index_in_dim(intersection_count, before, 0, keepdims=False)
    slots = jnp.arange(intersection_rows.shape[1], dtype=jnp.int32)
    lines = jnp.arange(FY, dtype=jnp.int32)
    row_keep = jnp.sum(
        ((listed[:, None] == lines[None, :]) & (slots[:, None] < in_use)).astype(F32), axis=0
    ) * (facet > 0).astype(F32)
    keep = jnp.broadcast_to(row_keep[None, :, None], (CH * POL, FY, MARGIN)).reshape(-1, MARGIN)

    return imaged(
        grids,
        jnp.asarray(row_table(), BF),
        jnp.cos(rad),
        jnp.sin(rad),
        jnp.cos(turn),
        jnp.sin(turn),
        keep,
    )


def solution(mesh):
    return jax.shard_map(
        shards,
        mesh=mesh,
        in_specs=(
            P(None, None, "chan", "facet"),
            P(),
            P(None, "facet"),
            P(None, None, "facet"),
            P(None, "facet"),
            P(),
            P(),
        ),
        out_specs=P("chan", None, None, "facet"),
        check_vma=False,
    )
```

```python
import math

import jax
import jax.numpy as jnp
import numpy as np
from jax import lax
from jax.experimental import pallas as pl
from jax.experimental.pallas import tpu as pltpu
from jax.sharding import PartitionSpec as P

BLK = 512
SG = 32
NSUB = 32
FX = 2048
FY = 64
MARGIN = 128
NX = 32768
GROUPS = 8
NB = 64
CH = 4
POL = 4
STAGES = 2
CPS = CH // STAGES
NL = CPS * POL * SG
RING = 4
BF = jnp.bfloat16
F32 = jnp.float32
MESH = pl.DeviceIdType.MESH


def plan_kernel(sub, out):
    lane = lax.broadcasted_iota(jnp.int32, (NB, 128), 1)
    line = lax.broadcasted_iota(jnp.int32, (NB, 128), 0)
    across = jnp.full((NB, 128), NSUB, jnp.int32)
    down = jnp.zeros((NB, 128), jnp.int32)
    for b in range(NB):
        value = sub[b // 8, b % 8]
        across = jnp.where(lane == b, value, across)
        down = jnp.where(line == b, value, down)
    ahead = (across < down) | ((across == down) & (lane < line))
    rank = jnp.sum(ahead.astype(jnp.int32), axis=1, keepdims=True)
    hit = rank == lane

    def total(x):
        return jnp.sum(x.astype(jnp.int32), axis=0, keepdims=True)

    order = total(jnp.where(hit, line, 0))
    placed = total(jnp.where(hit, down, 0))
    last = jnp.maximum(total(down <= lane) - 1, 0)
    has = jnp.minimum(total(down == lane), 1)
    earlier = pltpu.roll(jnp.broadcast_to(placed, (8, 128)), 1, 1)
    same = ((earlier[:1] == placed) & (lane[:1] > 0)).astype(jnp.int32)
    out[...] = jnp.concatenate([order, same, last, has] + [order] * 4, axis=0)


def sort_plan(block_sub):
    return pl.pallas_call(
        plan_kernel,
        out_shape=jax.ShapeDtypeStruct((8, 128), jnp.int32),
        in_specs=[pl.BlockSpec(memory_space=pltpu.SMEM)],
        out_specs=pl.BlockSpec(memory_space=pltpu.VMEM),
        name="sort_plan",
    )(block_sub)


def gather_kernel(
    vis,
    widx_h,
    offs_h,
    table,
    plan,
    grid_out,
    *scratch,
):
    recv = scratch[:STAGES]
    (
        widx,
        offs,
        left,
        right,
        pref,
        part,
        in1,
        mid,
        in2,
        local_sem,
        turn_send,
        turn_recv,
        own_sem,
        ring_send,
        ring_recv,
    ) = scratch[STAGES:]
    me = lax.axis_index("chan")
    facet = lax.axis_index("facet")
    mz = lax.div(facet, RING)
    mx = lax.rem(facet, RING)

    def x_peer(k):
        return lax.rem(mx + k, RING)

    def z_peer(k):
        return lax.rem(mz + k, RING)

    def on_x(x):
        return {"facet": mz * 4 + x}

    def on_z(z):
        return {"facet": z * 4 + mx}

    load_w = pltpu.make_async_copy(widx_h, widx, local_sem.at[0])
    load_o = pltpu.make_async_copy(offs_h, offs, local_sem.at[1])
    load_w.start()
    load_o.start()

    def block_refs(dest, source, st, blk):
        src = vis.at[pl.ds(dest * CH + st * CPS, CPS), :, pl.ds(blk * BLK, BLK)]
        return src, recv[st].at[source * 8 + blk]

    def slab(source, st):
        return recv[st].at[pl.ds(source * 8, 8)]

    for st in range(STAGES):
        for blk in range(8):
            src, dst = block_refs(me, me, st, blk)
            pltpu.make_async_copy(src, dst, own_sem.at[st]).start()

    barrier = pltpu.get_barrier_semaphore()
    for k in range(1, GROUPS):
        peer = lax.rem(me + k, GROUPS)
        pl.semaphore_signal(barrier, inc=1, device_id={"chan": peer}, device_id_type=MESH)
    for k in range(1, RING):
        pl.semaphore_signal(barrier, inc=1, device_id=on_x(x_peer(k)), device_id_type=MESH)
        pl.semaphore_signal(barrier, inc=1, device_id=on_z(z_peer(k)), device_id_type=MESH)
    pl.semaphore_wait(barrier, GROUPS - 1 + 2 * (RING - 1))

    for st in range(STAGES):
        for k in range(1, GROUPS):
            peer = lax.rem(me + k, GROUPS)
            for blk in range(8):
                src, dst = block_refs(peer, me, st, blk)
                pltpu.make_async_remote_copy(
                    src_ref=src,
                    dst_ref=dst,
                    send_sem=turn_send.at[st, k - 1],
                    recv_sem=turn_recv.at[st, k - 1],
                    device_id={"chan": peer},
                    device_id_type=MESH,
                ).start()

    def turned(st):
        mine = slab(me, st)
        pltpu.make_async_copy(mine, mine, own_sem.at[st]).wait()
        for k in range(1, GROUPS):
            peer = lax.rem(me + GROUPS - k, GROUPS)
            got = slab(peer, st)
            pltpu.make_async_remote_copy(
                src_ref=got,
                dst_ref=got,
                send_sem=turn_send.at[st, k - 1],
                recv_sem=turn_recv.at[st, k - 1],
                device_id={"chan": peer},
                device_id_type=MESH,
            ).wait()

    load_w.wait()
    load_o.wait()

    iota8 = lax.broadcasted_iota(jnp.int32, (8, 128), 0)
    blank = jnp.zeros((8, 128 - table.shape[2]), F32)
    tab_re = jnp.concatenate([table[0].astype(F32), blank], axis=1)
    tab_im = jnp.concatenate([table[1].astype(F32), blank], axis=1)

    def prep(tile, carry):
        lanes = pl.ds(pl.multiple_of(tile * 128, 128), 128)
        blk = lax.div(tile, 4)
        col = lax.rem(tile, 4) * 128
        cols = pl.ds(pl.multiple_of(col, 128), 128)
        cols_im = pl.ds(pl.multiple_of(col + BLK, 128), 128)
        planes = widx[:, lanes]
        offset = (offs[0, :, lanes], offs[1, :, lanes])
        for g in range(GROUPS):
            b = g * 8 + blk
            plane = jnp.broadcast_to(planes[g : g + 1], (8, 128))
            val_re = jnp.take_along_axis(tab_re, plane, axis=1)
            val_im = jnp.take_along_axis(tab_im, plane, axis=1)
            for side in range(2):
                off = jnp.broadcast_to(offset[side][g : g + 1], (8, 128))
                dist = iota8 - off
                cyc = lax.bitwise_and(dist, 7)
                tap_re = jnp.take_along_axis(val_re, cyc, axis=0)
                tap_im = jnp.take_along_axis(val_im, cyc, axis=0)
                res, ims = [], []
                for q in range(SG // 8):
                    ok = lax.bitwise_and(dist + 8 * q, -8) == 0
                    res.append(jnp.where(ok, tap_re, 0.0))
                    ims.append(jnp.where(ok, tap_im, 0.0))
                k_re = jnp.concatenate(res, axis=0)
                k_im = jnp.concatenate(ims, axis=0)
                if side == 0:
                    re16 = k_re.astype(BF)
                    left[b, 0:SG, cols] = re16
                    left[b, 0:SG, cols_im] = (-k_im).astype(BF)
                    left[b, SG : 2 * SG, cols] = k_im.astype(BF)
                    left[b, SG : 2 * SG, cols_im] = re16
                else:
                    right[b, 0, :, cols] = k_re
                    right[b, 1, :, cols] = k_im
        return carry

    lax.fori_loop(0, GROUPS * BLK // 128, prep, 0)

    def grid_part(st, lo, hi, run):
        def body(j, run):
            b = plan[0, j]
            kern = right[b]
            k_re = kern[0]
            k_im = kern[1]
            seen = recv[st][b]
            rows = []
            for c in range(CPS):
                v = seen[c].astype(F32)
                for p in range(POL):
                    v_re = jnp.broadcast_to(v[p : p + 1], (SG, BLK))
                    v_im = jnp.broadcast_to(v[p + POL : p + POL + 1], (SG, BLK))
                    y_re = (v_re * k_re - v_im * k_im).astype(BF)
                    y_im = (v_re * k_im + v_im * k_re).astype(BF)
                    rows.append(jnp.concatenate([y_re, y_im], axis=1))
            y = jnp.concatenate(rows, axis=0)
            o = lax.dot_general(
                left[b], y, (((1,), (1,)), ((), ())), preferred_element_type=F32
            )
            run = run * plan[1, j].astype(F32) + o
            pref[j] = run
            return run

        return lax.fori_loop(lo, hi, body, run, unroll=4)

    def emit(st):
        def body(s, carry):
            part[st, s] = (pref[plan[2, s]] * plan[3, s].astype(F32)).astype(BF)
            return carry

        lax.fori_loop(0, NSUB, body, 0)

    def ring_copy(st, half, phase, k, src, dst, dev):
        return pltpu.make_async_remote_copy(
            src_ref=src,
            dst_ref=dst,
            send_sem=ring_send.at[st, half, phase, k - 1],
            recv_sem=ring_recv.at[st, half, phase, k - 1],
            device_id=dev,
            device_id_type=MESH,
        )

    copies = {}
    half_n = NSUB // 2
    first = (mx, mz)
    second = (mz, mx)

    def dev_of(half, phase_axis, k):
        along_x = (half == 0) == (phase_axis == 0)
        return (x_peer(k), on_x(x_peer(k))) if along_x else (z_peer(k), on_z(z_peer(k)))

    def rs1(st):
        for half in range(2):
            for k in range(1, RING):
                pos, dev = dev_of(half, 0, k)
                cp = ring_copy(
                    st,
                    half,
                    0,
                    k,
                    part.at[st, pl.ds(half * half_n + 4 * pos, 4)],
                    in1.at[st, half, k - 1],
                    dev,
                )
                cp.start()
                copies[st, half, 0, k] = cp

    def rs2(st):
        for half in range(2):
            for k in range(1, RING):
                copies[st, half, 0, k].wait()
            total = part[st, pl.ds(half * half_n + 4 * first[half], 4)].astype(F32)
            for k in range(1, RING):
                total = total + in1[st, half, k - 1].astype(F32)
            mid[st, half] = total.astype(BF)
            for k in range(1, RING):
                pos, dev = dev_of(half, 1, k)
                cp = ring_copy(st, half, 1, k, mid.at[st, half, pos], in2.at[st, half, k - 1], dev)
                cp.start()
                copies[st, half, 1, k] = cp

    def ag1(st):
        for half in range(2):
            for k in range(1, RING):
                copies[st, half, 1, k].wait()
            total = mid[st, half, second[half]].astype(F32)
            for k in range(1, RING):
                total = total + in2[st, half, k - 1].astype(F32)
            slot = half * half_n + 4 * first[half] + second[half]
            grid_out[st, slot] = total.astype(BF)
            for k in range(1, RING):
                pos, dev = dev_of(half, 1, k)
                cp = ring_copy(
                    st, half, 2, k, grid_out.at[st, slot], grid_out.at[st, slot], dev
                )
                cp.start()
                copies[st, half, 2, k] = cp

    def ag2(st):
        for half in range(2):
            for k in range(1, RING):
                copies[st, half, 2, k].wait()
            span = pl.ds(half * half_n + 4 * first[half], 4)
            for k in range(1, RING):
                pos, dev = dev_of(half, 0, k)
                cp = ring_copy(
                    st, half, 3, k, grid_out.at[st, span], grid_out.at[st, span], dev
                )
                cp.start()
                copies[st, half, 3, k] = cp

    def finish(st):
        for half in range(2):
            for k in range(1, RING):
                copies[st, half, 3, k].wait()

    steps = []
    for st in range(STAGES):
        turned(st)
        run = jnp.zeros((2 * SG, NL), F32)
        for piece in range(4):
            run = grid_part(st, piece * (NB // 4), (piece + 1) * (NB // 4), run)
            if steps:
                steps.pop(0)()
        emit(st)
        rs1(st)
        steps += [
            (lambda st=st: rs2(st)),
            (lambda st=st: ag1(st)),
            (lambda st=st: ag2(st)),
            (lambda st=st: finish(st)),
        ]
    for step in steps:
        step()


def gridded(vis, w_index, offsets, table, plan):
    any_spec = pl.BlockSpec(memory_space=pl.ANY)
    vmem = pl.BlockSpec(memory_space=pltpu.VMEM)
    smem = pl.BlockSpec(memory_space=pltpu.SMEM)
    return pl.pallas_call(
        gather_kernel,
        out_shape=jax.ShapeDtypeStruct((STAGES, NSUB, 2 * SG, NL), BF),
        in_specs=[any_spec, any_spec, any_spec, vmem, smem],
        out_specs=vmem,
        scratch_shapes=[
            *[pltpu.VMEM((NB, CPS, 2 * POL, BLK), BF)] * STAGES,
            pltpu.VMEM((GROUPS, GROUPS * BLK), jnp.int32),
            pltpu.VMEM((2, GROUPS, GROUPS * BLK), jnp.int32),
            pltpu.VMEM((NB, 2 * SG, 2 * BLK), BF),
            pltpu.VMEM((NB, 2, SG, BLK), F32),
            pltpu.VMEM((NB, 2 * SG, NL), F32),
            pltpu.VMEM((STAGES, NSUB, 2 * SG, NL), BF),
            pltpu.VMEM((STAGES, 2, RING - 1, 4, 2 * SG, NL), BF),
            pltpu.VMEM((STAGES, 2, 4, 2 * SG, NL), BF),
            pltpu.VMEM((STAGES, 2, RING - 1, 2 * SG, NL), BF),
            pltpu.SemaphoreType.DMA((2,)),
            pltpu.SemaphoreType.DMA((STAGES, GROUPS - 1)),
            pltpu.SemaphoreType.DMA((STAGES, GROUPS - 1)),
            pltpu.SemaphoreType.DMA((STAGES,)),
            pltpu.SemaphoreType.DMA((STAGES, 2, 4, RING - 1)),
            pltpu.SemaphoreType.DMA((STAGES, 2, 4, RING - 1)),
        ],
        compiler_params=pltpu.CompilerParams(
            collective_id=0, has_side_effects=True, vmem_limit_bytes=60 * 2**20
        ),
        name="turn_grid_share",
    )(vis, w_index, offsets, table, plan)


XT = 256
NT = FX // XT
KH = NSUB * SG
KQ = 128


def image_kernel(rows_s, count_s, grids, row_tab, base, cells, spin, shift, out, z, col, edge, cur):
    step = pl.program_id(0)

    def fill(width):
        for q in range(KH // KQ):
            rows = pl.ds(q * KQ, KQ)
            turn = pl.ds((q % 2) * KQ, KQ)
            wc = spin[0, turn]
            ws = spin[1, turn]
            c = cur[0, rows]
            s = cur[1, rows]
            for h in range(width // 128):
                col[pl.ds(q * 2 * KQ, KQ), pl.ds(h * 128, 128)] = c.astype(BF)
                col[pl.ds(q * 2 * KQ + KQ, KQ), pl.ds(h * 128, 128)] = (-s).astype(BF)
                c, s = c * wc - s * ws, s * wc + c * ws
            cur[0, rows] = c
            cur[1, rows] = s

    @pl.when(step == 0)
    def _():
        img_scale = 1.0 / math.sqrt(GROUPS * 65536)
        facet = lax.axis_index("facet")

        def rows4(q, carry):
            for st in range(STAGES):
                os = []
                for gi in range(4):
                    g = q * 4 + gi
                    os.append(
                        jnp.dot(row_tab[g], grids[st, g], preferred_element_type=F32) * img_scale
                    )
                for c in range(CPS):
                    for p in range(POL):
                        lo = c * POL * SG + p * SG
                        both = jnp.concatenate([o[:, lo : lo + SG] for o in os], axis=1).astype(BF)
                        at = (st * CPS + c) * POL * FY + p * FY
                        lanes0 = pl.ds(pl.multiple_of(q * 256, 128), 128)
                        lanes1 = pl.ds(pl.multiple_of(q * 256 + 128, 128), 128)
                        z[pl.ds(at, FY), lanes0] = both[:FY]
                        z[pl.ds(at, FY), lanes1] = both[FY:]
            return carry

        lax.fori_loop(0, NSUB // 4, rows4, 0)

        fc = shift[0, facet]
        fs = shift[1, facet]
        vc = jnp.concatenate([fc, fc], axis=0)
        vs = jnp.concatenate([fs, fs], axis=0)
        cell_c = cells[0] * vc - cells[1] * vs
        cell_s = cells[1] * vc + cells[0] * vs
        for g in range(NSUB):
            rows = pl.ds(g * SG, SG)
            c = base[0, g : g + 1]
            s = base[1, g : g + 1]
            cur[0, rows] = cell_c * c - cell_s * s
            cur[1, rows] = cell_s * c + cell_c * s

        fill(128)
        before = jnp.maximum(facet - 1, 0)
        lines = lax.broadcasted_iota(jnp.int32, (FY, MARGIN), 0)
        used = jnp.where(facet > 0, count_s[before], 0)
        keep = jnp.zeros((FY, MARGIN), F32)
        for slot in range(32):
            row = jnp.where(slot < used, rows_s[before, slot], -1)
            keep = keep + jnp.where(lines == row, 1.0, 0.0)
        prev = jnp.dot(z[...], col[:, 0:128], preferred_element_type=F32)
        edge[...] = prev.reshape(CH, POL, FY, MARGIN) * keep

    fill(XT)
    o = jnp.dot(z[...], col[...], preferred_element_type=F32)
    out[...] = o.reshape(CH, POL, FY, XT)

    @pl.when(step == 0)
    def _():
        out[:, :, :, 0:MARGIN] = out[:, :, :, 0:MARGIN] + edge[...]


def imaged(grids, rows_list, counts, *tables):
    def whole(shape):
        return pl.BlockSpec(shape, lambda n: (0,) * len(shape), pipeline_mode=pl.Buffered(1))

    smem = pl.BlockSpec(memory_space=pltpu.SMEM)
    return pl.pallas_call(
        image_kernel,
        grid=(NT,),
        out_shape=jax.ShapeDtypeStruct((CH, POL, FY, FX), F32),
        in_specs=[smem, smem]
        + [whole(a.shape) for a in (grids, *tables)],
        out_specs=pl.BlockSpec((CH, POL, FY, XT), lambda n: (0, 0, 0, n)),
        scratch_shapes=[
            pltpu.VMEM((CH * POL * FY, KH * 2), BF),
            pltpu.VMEM((KH * 2, XT), BF),
            pltpu.VMEM((CH, POL, FY, MARGIN), F32),
            pltpu.VMEM((2, KH, 128), F32),
        ],
        compiler_params=pltpu.CompilerParams(vmem_limit_bytes=60 * 2**20),
        name="facet_image",
    )(rows_list, counts, grids, *tables)


def waves(turns, period):
    rad = np.mod(turns, period).astype(np.float64) * (2.0 * math.pi / period)
    return jnp.asarray(np.stack([np.cos(rad), np.sin(rad)]), F32)


def row_table():
    g = np.arange(NSUB)
    span = NX // SG
    anchor = ((37 * g) % span - span // 2) * SG
    lines = np.arange(FY) - FY // 2
    phase = ((anchor[:, None, None] + np.arange(SG)[None, None, :]) * lines[None, :, None]) % NX
    rad = phase.astype(np.float32) * np.float32(2.0 * math.pi / NX)
    cos, sin = np.cos(rad), np.sin(rad)
    top = np.concatenate([cos, -sin], axis=2)
    low = np.concatenate([sin, cos], axis=2)
    return np.concatenate([top, low], axis=1)


def shards(
    visibilities, w_kernel, w_index, cell_offsets, block_sub, intersection_rows, intersection_count
):
    vis = visibilities.reshape(visibilities.shape[0], 2 * POL, w_index.shape[1])
    table = w_kernel.transpose(1, 2, 0)
    grids = gridded(vis, w_index, cell_offsets, table, sort_plan(block_sub))

    g = np.arange(NSUB)
    span = NX // SG
    anchor = ((53 * g + 5) % span - span // 2) * SG
    freq = (anchor[:, None] + np.arange(SG)[None, :]).reshape(-1, 1)
    x = -NX // 2 - MARGIN + np.arange(128)[None, :]
    ones = np.ones((1, 128), np.int64)
    half = np.arange(16)[:, None]
    base = waves(anchor[:, None] * x, NX)
    cells = waves(np.arange(SG)[:, None] * x, NX)
    spin = waves(freq[: 2 * KQ] * 128 * ones, NX)
    shift = waves(np.arange(NX // FX)[:, None, None] * FX * half[None] * ones, NX)
    assert np.all((freq.reshape(-1, 2 * KQ) * 128 - freq[: 2 * KQ].T * 128) % NX == 0)

    return imaged(
        grids,
        intersection_rows,
        intersection_count,
        jnp.asarray(row_table(), BF),
        base,
        cells,
        spin,
        shift,
    )


def solution(mesh):
    return jax.shard_map(
        shards,
        mesh=mesh,
        in_specs=(
            P(None, None, "chan", "facet"),
            P(),
            P(None, "facet"),
            P(None, None, "facet"),
            P(None, "facet"),
            P(),
            P(),
        ),
        out_specs=P("chan", None, None, "facet"),
        check_vma=False,
    )
```

```python
import math

import jax
import jax.numpy as jnp
import numpy as np
from jax import lax
from jax.experimental import pallas as pl
from jax.experimental.pallas import tpu as pltpu
from jax.sharding import PartitionSpec as P

BLK = 512
SG = 32
NSUB = 32
FX = 2048
FY = 64
MARGIN = 128
NX = 32768
GROUPS = 8
NB = 64
CH = 4
POL = 4
STAGES = 4
CPS = CH // STAGES
NL = CPS * POL * SG
RING = 4
BF = jnp.bfloat16
F32 = jnp.float32
MESH = pl.DeviceIdType.MESH


def plan_kernel(sub, out):
    lane = lax.broadcasted_iota(jnp.int32, (NB, 128), 1)
    line = lax.broadcasted_iota(jnp.int32, (NB, 128), 0)
    across = jnp.full((NB, 128), NSUB, jnp.int32)
    down = jnp.zeros((NB, 128), jnp.int32)
    for b in range(NB):
        value = sub[b // 8, b % 8]
        across = jnp.where(lane == b, value, across)
        down = jnp.where(line == b, value, down)
    ahead = (across < down) | ((across == down) & (lane < line))
    rank = jnp.sum(ahead.astype(jnp.int32), axis=1, keepdims=True)
    hit = rank == lane

    def total(x):
        return jnp.sum(x.astype(jnp.int32), axis=0, keepdims=True)

    order = total(jnp.where(hit, line, 0))
    placed = total(jnp.where(hit, down, 0))
    last = jnp.maximum(total(down <= lane) - 1, 0)
    has = jnp.minimum(total(down == lane), 1)
    earlier = pltpu.roll(jnp.broadcast_to(placed, (8, 128)), 1, 1)
    same = ((earlier[:1] == placed) & (lane[:1] > 0)).astype(jnp.int32)
    out[...] = jnp.concatenate([order, same, last, has] + [order] * 4, axis=0)


def sort_plan(block_sub):
    return pl.pallas_call(
        plan_kernel,
        out_shape=jax.ShapeDtypeStruct((8, 128), jnp.int32),
        in_specs=[pl.BlockSpec(memory_space=pltpu.SMEM)],
        out_specs=pl.BlockSpec(memory_space=pltpu.VMEM),
        name="sort_plan",
    )(block_sub)


def gather_kernel(
    vis,
    widx_h,
    offs_h,
    table,
    plan,
    grid_out,
    *scratch,
):
    recv = scratch[:STAGES]
    (
        widx,
        offs,
        left,
        right,
        pref,
        part,
        in1,
        mid,
        in2,
        local_sem,
        turn_send,
        turn_recv,
        own_sem,
        ring_send,
        ring_recv,
    ) = scratch[STAGES:]
    me = lax.axis_index("chan")
    facet = lax.axis_index("facet")
    mz = lax.div(facet, RING)
    mx = lax.rem(facet, RING)

    def x_peer(k):
        return lax.rem(mx + k, RING)

    def z_peer(k):
        return lax.rem(mz + k, RING)

    def on_x(x):
        return {"facet": mz * 4 + x}

    def on_z(z):
        return {"facet": z * 4 + mx}

    load_w = pltpu.make_async_copy(widx_h, widx, local_sem.at[0])
    load_o = pltpu.make_async_copy(offs_h, offs, local_sem.at[1])
    load_w.start()
    load_o.start()

    def block_refs(dest, source, st, blk):
        src = vis.at[pl.ds(dest * CH + st * CPS, CPS), :, pl.ds(blk * BLK, BLK)]
        return src, recv[st].at[source * 8 + blk]

    def slab(source, st):
        return recv[st].at[pl.ds(source * 8, 8)]

    for st in range(STAGES):
        for blk in range(8):
            src, dst = block_refs(me, me, st, blk)
            pltpu.make_async_copy(src, dst, own_sem.at[st]).start()

    barrier = pltpu.get_barrier_semaphore()
    for k in range(1, GROUPS):
        peer = lax.rem(me + k, GROUPS)
        pl.semaphore_signal(barrier, inc=1, device_id={"chan": peer}, device_id_type=MESH)
    for k in range(1, RING):
        pl.semaphore_signal(barrier, inc=1, device_id=on_x(x_peer(k)), device_id_type=MESH)
        pl.semaphore_signal(barrier, inc=1, device_id=on_z(z_peer(k)), device_id_type=MESH)
    pl.semaphore_wait(barrier, GROUPS - 1 + 2 * (RING - 1))

    for st in range(STAGES):
        for k in range(1, GROUPS):
            peer = lax.rem(me + k, GROUPS)
            for blk in range(8):
                src, dst = block_refs(peer, me, st, blk)
                pltpu.make_async_remote_copy(
                    src_ref=src,
                    dst_ref=dst,
                    send_sem=turn_send.at[st, k - 1],
                    recv_sem=turn_recv.at[st, k - 1],
                    device_id={"chan": peer},
                    device_id_type=MESH,
                ).start()

    def turned(st):
        mine = slab(me, st)
        pltpu.make_async_copy(mine, mine, own_sem.at[st]).wait()
        for k in range(1, GROUPS):
            peer = lax.rem(me + GROUPS - k, GROUPS)
            got = slab(peer, st)
            pltpu.make_async_remote_copy(
                src_ref=got,
                dst_ref=got,
                send_sem=turn_send.at[st, k - 1],
                recv_sem=turn_recv.at[st, k - 1],
                device_id={"chan": peer},
                device_id_type=MESH,
            ).wait()

    load_w.wait()
    load_o.wait()

    iota8 = lax.broadcasted_iota(jnp.int32, (8, 128), 0)
    blank = jnp.zeros((8, 128 - table.shape[2]), F32)
    tab_re = jnp.concatenate([table[0].astype(F32), blank], axis=1)
    tab_im = jnp.concatenate([table[1].astype(F32), blank], axis=1)

    def prep(tile, carry):
        lanes = pl.ds(pl.multiple_of(tile * 128, 128), 128)
        blk = lax.div(tile, 4)
        col = lax.rem(tile, 4) * 128
        cols = pl.ds(pl.multiple_of(col, 128), 128)
        cols_im = pl.ds(pl.multiple_of(col + BLK, 128), 128)
        planes = widx[:, lanes]
        offset = (offs[0, :, lanes], offs[1, :, lanes])
        for g in range(GROUPS):
            b = g * 8 + blk
            plane = jnp.broadcast_to(planes[g : g + 1], (8, 128))
            val_re = jnp.take_along_axis(tab_re, plane, axis=1)
            val_im = jnp.take_along_axis(tab_im, plane, axis=1)
            for side in range(2):
                off = jnp.broadcast_to(offset[side][g : g + 1], (8, 128))
                dist = iota8 - off
                cyc = lax.bitwise_and(dist, 7)
                tap_re = jnp.take_along_axis(val_re, cyc, axis=0)
                tap_im = jnp.take_along_axis(val_im, cyc, axis=0)
                res, ims = [], []
                for q in range(SG // 8):
                    ok = lax.bitwise_and(dist + 8 * q, -8) == 0
                    res.append(jnp.where(ok, tap_re, 0.0))
                    ims.append(jnp.where(ok, tap_im, 0.0))
                k_re = jnp.concatenate(res, axis=0)
                k_im = jnp.concatenate(ims, axis=0)
                if side == 0:
                    re16 = k_re.astype(BF)
                    left[b, 0:SG, cols] = re16
                    left[b, 0:SG, cols_im] = (-k_im).astype(BF)
                    left[b, SG : 2 * SG, cols] = k_im.astype(BF)
                    left[b, SG : 2 * SG, cols_im] = re16
                else:
                    right[b, 0, :, cols] = k_re
                    right[b, 1, :, cols] = k_im
        return carry

    lax.fori_loop(0, GROUPS * BLK // 128, prep, 0)

    def grid_part(st, lo, hi, run):
        def body(j, run):
            b = plan[0, j]
            kern = right[b]
            k_re = kern[0]
            k_im = kern[1]
            seen = recv[st][b]
            rows = []
            for c in range(CPS):
                v = seen[c].astype(F32)
                for p in range(POL):
                    v_re = jnp.broadcast_to(v[p : p + 1], (SG, BLK))
                    v_im = jnp.broadcast_to(v[p + POL : p + POL + 1], (SG, BLK))
                    y_re = (v_re * k_re - v_im * k_im).astype(BF)
                    y_im = (v_re * k_im + v_im * k_re).astype(BF)
                    rows.append(jnp.concatenate([y_re, y_im], axis=1))
            y = jnp.concatenate(rows, axis=0)
            o = lax.dot_general(
                left[b], y, (((1,), (1,)), ((), ())), preferred_element_type=F32
            )
            run = run * plan[1, j].astype(F32) + o
            pref[j] = run
            return run

        return lax.fori_loop(lo, hi, body, run, unroll=4)

    def emit(st):
        def body(s, carry):
            part[st, s] = (pref[plan[2, s]] * plan[3, s].astype(F32)).astype(BF)
            return carry

        lax.fori_loop(0, NSUB, body, 0)

    def ring_copy(st, half, phase, k, src, dst, dev):
        return pltpu.make_async_remote_copy(
            src_ref=src,
            dst_ref=dst,
            send_sem=ring_send.at[st, half, phase, k - 1],
            recv_sem=ring_recv.at[st, half, phase, k - 1],
            device_id=dev,
            device_id_type=MESH,
        )

    copies = {}
    half_n = NSUB // 2
    first = (mx, mz)
    second = (mz, mx)

    def dev_of(half, phase_axis, k):
        along_x = (half == 0) == (phase_axis == 0)
        return (x_peer(k), on_x(x_peer(k))) if along_x else (z_peer(k), on_z(z_peer(k)))

    def rs1(st):
        for half in range(2):
            for k in range(1, RING):
                pos, dev = dev_of(half, 0, k)
                cp = ring_copy(
                    st,
                    half,
                    0,
                    k,
                    part.at[st, pl.ds(half * half_n + 4 * pos, 4)],
                    in1.at[st, half, k - 1],
                    dev,
                )
                cp.start()
                copies[st, half, 0, k] = cp

    def rs2(st):
        for half in range(2):
            for k in range(1, RING):
                copies[st, half, 0, k].wait()
            total = part[st, pl.ds(half * half_n + 4 * first[half], 4)].astype(F32)
            for k in range(1, RING):
                total = total + in1[st, half, k - 1].astype(F32)
            mid[st, half] = total.astype(BF)
            for k in range(1, RING):
                pos, dev = dev_of(half, 1, k)
                cp = ring_copy(st, half, 1, k, mid.at[st, half, pos], in2.at[st, half, k - 1], dev)
                cp.start()
                copies[st, half, 1, k] = cp

    def ag1(st):
        for half in range(2):
            for k in range(1, RING):
                copies[st, half, 1, k].wait()
            total = mid[st, half, second[half]].astype(F32)
            for k in range(1, RING):
                total = total + in2[st, half, k - 1].astype(F32)
            slot = half * half_n + 4 * first[half] + second[half]
            grid_out[st, slot] = total.astype(BF)
            for k in range(1, RING):
                pos, dev = dev_of(half, 1, k)
                cp = ring_copy(
                    st, half, 2, k, grid_out.at[st, slot], grid_out.at[st, slot], dev
                )
                cp.start()
                copies[st, half, 2, k] = cp

    def ag2(st):
        for half in range(2):
            for k in range(1, RING):
                copies[st, half, 2, k].wait()
            span = pl.ds(half * half_n + 4 * first[half], 4)
            for k in range(1, RING):
                pos, dev = dev_of(half, 0, k)
                cp = ring_copy(
                    st, half, 3, k, grid_out.at[st, span], grid_out.at[st, span], dev
                )
                cp.start()
                copies[st, half, 3, k] = cp

    def finish(st):
        for half in range(2):
            for k in range(1, RING):
                copies[st, half, 3, k].wait()

    pending = []

    def advance():
        for todo in pending:
            todo.pop(0)()
        pending[:] = [todo for todo in pending if todo]

    for st in range(STAGES):
        turned(st)
        run = jnp.zeros((2 * SG, NL), F32)
        for piece in range(2):
            run = grid_part(st, piece * (NB // 2), (piece + 1) * (NB // 2), run)
            advance()
        emit(st)
        rs1(st)
        pending.append([lambda st=st, f=f: f(st) for f in (rs2, ag1, ag2, finish)])
    while pending:
        advance()


def gridded(vis, w_index, offsets, table, plan):
    any_spec = pl.BlockSpec(memory_space=pl.ANY)
    vmem = pl.BlockSpec(memory_space=pltpu.VMEM)
    smem = pl.BlockSpec(memory_space=pltpu.SMEM)
    return pl.pallas_call(
        gather_kernel,
        out_shape=jax.ShapeDtypeStruct((STAGES, NSUB, 2 * SG, NL), BF),
        in_specs=[any_spec, any_spec, any_spec, vmem, smem],
        out_specs=vmem,
        scratch_shapes=[
            *[pltpu.VMEM((NB, CPS, 2 * POL, BLK), BF)] * STAGES,
            pltpu.VMEM((GROUPS, GROUPS * BLK), jnp.int32),
            pltpu.VMEM((2, GROUPS, GROUPS * BLK), jnp.int32),
            pltpu.VMEM((NB, 2 * SG, 2 * BLK), BF),
            pltpu.VMEM((NB, 2, SG, BLK), F32),
            pltpu.VMEM((NB, 2 * SG, NL), F32),
            pltpu.VMEM((STAGES, NSUB, 2 * SG, NL), BF),
            pltpu.VMEM((STAGES, 2, RING - 1, 4, 2 * SG, NL), BF),
            pltpu.VMEM((STAGES, 2, 4, 2 * SG, NL), BF),
            pltpu.VMEM((STAGES, 2, RING - 1, 2 * SG, NL), BF),
            pltpu.SemaphoreType.DMA((2,)),
            pltpu.SemaphoreType.DMA((STAGES, GROUPS - 1)),
            pltpu.SemaphoreType.DMA((STAGES, GROUPS - 1)),
            pltpu.SemaphoreType.DMA((STAGES,)),
            pltpu.SemaphoreType.DMA((STAGES, 2, 4, RING - 1)),
            pltpu.SemaphoreType.DMA((STAGES, 2, 4, RING - 1)),
        ],
        compiler_params=pltpu.CompilerParams(
            collective_id=0, has_side_effects=True, vmem_limit_bytes=60 * 2**20
        ),
        name="turn_grid_share",
    )(vis, w_index, offsets, table, plan)


XT = 256
NT = FX // XT
KH = NSUB * SG
KQ = 128


def image_kernel(rows_s, count_s, grids, row_tab, base, cells, spin, shift, out, z, col, edge, cur):
    step = pl.program_id(0)

    def fill(width):
        for q in range(KH // KQ):
            rows = pl.ds(q * KQ, KQ)
            turn = pl.ds((q % 2) * KQ, KQ)
            wc = spin[0, turn]
            ws = spin[1, turn]
            c = cur[0, rows]
            s = cur[1, rows]
            for h in range(width // 128):
                col[pl.ds(q * 2 * KQ, KQ), pl.ds(h * 128, 128)] = c.astype(BF)
                col[pl.ds(q * 2 * KQ + KQ, KQ), pl.ds(h * 128, 128)] = (-s).astype(BF)
                c, s = c * wc - s * ws, s * wc + c * ws
            cur[0, rows] = c
            cur[1, rows] = s

    @pl.when(step == 0)
    def _():
        img_scale = 1.0 / math.sqrt(GROUPS * 65536)
        facet = lax.axis_index("facet")

        def rows4(q, carry):
            for st in range(STAGES):
                os = []
                for gi in range(4):
                    g = q * 4 + gi
                    os.append(
                        jnp.dot(row_tab[g], grids[st, g], preferred_element_type=F32) * img_scale
                    )
                for c in range(CPS):
                    for p in range(POL):
                        lo = c * POL * SG + p * SG
                        both = jnp.concatenate([o[:, lo : lo + SG] for o in os], axis=1).astype(BF)
                        at = (st * CPS + c) * POL * FY + p * FY
                        lanes0 = pl.ds(pl.multiple_of(q * 256, 128), 128)
                        lanes1 = pl.ds(pl.multiple_of(q * 256 + 128, 128), 128)
                        z[pl.ds(at, FY), lanes0] = both[:FY]
                        z[pl.ds(at, FY), lanes1] = both[FY:]
            return carry

        lax.fori_loop(0, NSUB // 4, rows4, 0)

        fc = shift[0, facet]
        fs = shift[1, facet]
        vc = jnp.concatenate([fc, fc], axis=0)
        vs = jnp.concatenate([fs, fs], axis=0)
        cell_c = cells[0] * vc - cells[1] * vs
        cell_s = cells[1] * vc + cells[0] * vs
        for g in range(NSUB):
            rows = pl.ds(g * SG, SG)
            c = base[0, g : g + 1]
            s = base[1, g : g + 1]
            cur[0, rows] = cell_c * c - cell_s * s
            cur[1, rows] = cell_s * c + cell_c * s

        fill(128)
        before = jnp.maximum(facet - 1, 0)
        lines = lax.broadcasted_iota(jnp.int32, (FY, MARGIN), 0)
        used = jnp.where(facet > 0, count_s[before], 0)
        keep = jnp.zeros((FY, MARGIN), F32)
        for slot in range(32):
            row = jnp.where(slot < used, rows_s[before, slot], -1)
            keep = keep + jnp.where(lines == row, 1.0, 0.0)
        prev = jnp.dot(z[...], col[:, 0:128], preferred_element_type=F32)
        edge[...] = prev.reshape(CH, POL, FY, MARGIN) * keep

    fill(XT)
    o = jnp.dot(z[...], col[...], preferred_element_type=F32)
    out[...] = o.reshape(CH, POL, FY, XT)

    @pl.when(step == 0)
    def _():
        out[:, :, :, 0:MARGIN] = out[:, :, :, 0:MARGIN] + edge[...]


def imaged(grids, rows_list, counts, *tables):
    def whole(shape):
        return pl.BlockSpec(shape, lambda n: (0,) * len(shape), pipeline_mode=pl.Buffered(1))

    smem = pl.BlockSpec(memory_space=pltpu.SMEM)
    return pl.pallas_call(
        image_kernel,
        grid=(NT,),
        out_shape=jax.ShapeDtypeStruct((CH, POL, FY, FX), F32),
        in_specs=[smem, smem]
        + [whole(a.shape) for a in (grids, *tables)],
        out_specs=pl.BlockSpec((CH, POL, FY, XT), lambda n: (0, 0, 0, n)),
        scratch_shapes=[
            pltpu.VMEM((CH * POL * FY, KH * 2), BF),
            pltpu.VMEM((KH * 2, XT), BF),
            pltpu.VMEM((CH, POL, FY, MARGIN), F32),
            pltpu.VMEM((2, KH, 128), F32),
        ],
        compiler_params=pltpu.CompilerParams(vmem_limit_bytes=60 * 2**20),
        name="facet_image",
    )(rows_list, counts, grids, *tables)


def waves(turns, period):
    rad = np.mod(turns, period).astype(np.float64) * (2.0 * math.pi / period)
    return jnp.asarray(np.stack([np.cos(rad), np.sin(rad)]), F32)


def row_table():
    g = np.arange(NSUB)
    span = NX // SG
    anchor = ((37 * g) % span - span // 2) * SG
    lines = np.arange(FY) - FY // 2
    phase = ((anchor[:, None, None] + np.arange(SG)[None, None, :]) * lines[None, :, None]) % NX
    rad = phase.astype(np.float32) * np.float32(2.0 * math.pi / NX)
    cos, sin = np.cos(rad), np.sin(rad)
    top = np.concatenate([cos, -sin], axis=2)
    low = np.concatenate([sin, cos], axis=2)
    return np.concatenate([top, low], axis=1)


def shards(
    visibilities, w_kernel, w_index, cell_offsets, block_sub, intersection_rows, intersection_count
):
    vis = visibilities.reshape(visibilities.shape[0], 2 * POL, w_index.shape[1])
    table = w_kernel.transpose(1, 2, 0)
    grids = gridded(vis, w_index, cell_offsets, table, sort_plan(block_sub))

    g = np.arange(NSUB)
    span = NX // SG
    anchor = ((53 * g + 5) % span - span // 2) * SG
    freq = (anchor[:, None] + np.arange(SG)[None, :]).reshape(-1, 1)
    x = -NX // 2 - MARGIN + np.arange(128)[None, :]
    ones = np.ones((1, 128), np.int64)
    half = np.arange(16)[:, None]
    base = waves(anchor[:, None] * x, NX)
    cells = waves(np.arange(SG)[:, None] * x, NX)
    spin = waves(freq[: 2 * KQ] * 128 * ones, NX)
    shift = waves(np.arange(NX // FX)[:, None, None] * FX * half[None] * ones, NX)
    assert np.all((freq.reshape(-1, 2 * KQ) * 128 - freq[: 2 * KQ].T * 128) % NX == 0)

    return imaged(
        grids,
        intersection_rows,
        intersection_count,
        jnp.asarray(row_table(), BF),
        base,
        cells,
        spin,
        shift,
    )


def solution(mesh):
    return jax.shard_map(
        shards,
        mesh=mesh,
        in_specs=(
            P(None, None, "chan", "facet"),
            P(),
            P(None, "facet"),
            P(None, None, "facet"),
            P(None, "facet"),
            P(),
            P(),
        ),
        out_specs=P("chan", None, None, "facet"),
        check_vma=False,
    )
```

```python
import math

import jax
import jax.numpy as jnp
import numpy as np
from jax import lax
from jax.experimental import pallas as pl
from jax.experimental.pallas import tpu as pltpu
from jax.sharding import PartitionSpec as P

BLK = 512
SG = 32
NSUB = 32
FX = 2048
FY = 64
MARGIN = 128
NX = 32768
GROUPS = 8
NB = 64
CH = 4
POL = 4
STAGES = 4
CPS = CH // STAGES
NL = CPS * POL * SG
RING = 4
BF = jnp.bfloat16
F32 = jnp.float32
MESH = pl.DeviceIdType.MESH


def plan_kernel(sub, out):
    lane = lax.broadcasted_iota(jnp.int32, (NB, 128), 1)
    line = lax.broadcasted_iota(jnp.int32, (NB, 128), 0)
    across = jnp.full((NB, 128), NSUB, jnp.int32)
    down = jnp.zeros((NB, 128), jnp.int32)
    for b in range(NB):
        value = sub[b // 8, b % 8]
        across = jnp.where(lane == b, value, across)
        down = jnp.where(line == b, value, down)
    ahead = (across < down) | ((across == down) & (lane < line))
    rank = jnp.sum(ahead.astype(jnp.int32), axis=1, keepdims=True)
    hit = rank == lane

    def total(x):
        return jnp.sum(x.astype(jnp.int32), axis=0, keepdims=True)

    order = total(jnp.where(hit, line, 0))
    placed = total(jnp.where(hit, down, 0))
    last = jnp.maximum(total(down <= lane) - 1, 0)
    has = jnp.minimum(total(down == lane), 1)
    earlier = pltpu.roll(jnp.broadcast_to(placed, (8, 128)), 1, 1)
    same = ((earlier[:1] == placed) & (lane[:1] > 0)).astype(jnp.int32)
    out[...] = jnp.concatenate([order, same, last, has] + [order] * 4, axis=0)


def sort_plan(block_sub):
    return pl.pallas_call(
        plan_kernel,
        out_shape=jax.ShapeDtypeStruct((8, 128), jnp.int32),
        in_specs=[pl.BlockSpec(memory_space=pltpu.SMEM)],
        out_specs=pl.BlockSpec(memory_space=pltpu.VMEM),
        name="sort_plan",
    )(block_sub)


def gather_kernel(
    vis,
    widx_h,
    offs_h,
    table,
    plan,
    grid_out,
    *scratch,
):
    recv = scratch[:STAGES]
    (
        widx,
        offs,
        left,
        right,
        pref,
        part,
        in1,
        mid,
        in2,
        local_sem,
        turn_send,
        turn_recv,
        own_sem,
        ring_send,
        ring_recv,
    ) = scratch[STAGES:]
    me = lax.axis_index("chan")
    facet = lax.axis_index("facet")
    mz = lax.div(facet, RING)
    mx = lax.rem(facet, RING)

    def x_peer(k):
        return lax.rem(mx + k, RING)

    def z_peer(k):
        return lax.rem(mz + k, RING)

    def on_x(x):
        return {"facet": mz * 4 + x}

    def on_z(z):
        return {"facet": z * 4 + mx}

    load_w = pltpu.make_async_copy(widx_h, widx, local_sem.at[0])
    load_o = pltpu.make_async_copy(offs_h, offs, local_sem.at[1])
    load_w.start()
    load_o.start()

    def block_refs(dest, source, st, blk):
        src = vis.at[pl.ds(dest * CH + st * CPS, CPS), :, pl.ds(blk * BLK, BLK)]
        return src, recv[st].at[source * 8 + blk]

    def slab(source, st):
        return recv[st].at[pl.ds(source * 8, 8)]

    for st in range(STAGES):
        for blk in range(8):
            src, dst = block_refs(me, me, st, blk)
            pltpu.make_async_copy(src, dst, own_sem.at[st]).start()

    barrier = pltpu.get_barrier_semaphore()
    for k in range(1, GROUPS):
        peer = lax.rem(me + k, GROUPS)
        pl.semaphore_signal(barrier, inc=1, device_id={"chan": peer}, device_id_type=MESH)
    for k in range(1, RING):
        pl.semaphore_signal(barrier, inc=1, device_id=on_x(x_peer(k)), device_id_type=MESH)
        pl.semaphore_signal(barrier, inc=1, device_id=on_z(z_peer(k)), device_id_type=MESH)
    pl.semaphore_wait(barrier, GROUPS - 1 + 2 * (RING - 1))

    for st in range(STAGES):
        for k in range(1, GROUPS):
            peer = lax.rem(me + k, GROUPS)
            for blk in range(8):
                src, dst = block_refs(peer, me, st, blk)
                pltpu.make_async_remote_copy(
                    src_ref=src,
                    dst_ref=dst,
                    send_sem=turn_send.at[st, k - 1],
                    recv_sem=turn_recv.at[st, k - 1],
                    device_id={"chan": peer},
                    device_id_type=MESH,
                ).start()

    def turned(st):
        mine = slab(me, st)
        pltpu.make_async_copy(mine, mine, own_sem.at[st]).wait()
        for k in range(1, GROUPS):
            peer = lax.rem(me + GROUPS - k, GROUPS)
            got = slab(peer, st)
            pltpu.make_async_remote_copy(
                src_ref=got,
                dst_ref=got,
                send_sem=turn_send.at[st, k - 1],
                recv_sem=turn_recv.at[st, k - 1],
                device_id={"chan": peer},
                device_id_type=MESH,
            ).wait()

    load_w.wait()
    load_o.wait()

    iota8 = lax.broadcasted_iota(jnp.int32, (8, 128), 0)
    blank = jnp.zeros((8, 128 - table.shape[2]), F32)
    tab_re = jnp.concatenate([table[0].astype(F32), blank], axis=1)
    tab_im = jnp.concatenate([table[1].astype(F32), blank], axis=1)

    def prep(tile, carry):
        lanes = pl.ds(pl.multiple_of(tile * 128, 128), 128)
        blk = lax.div(tile, 4)
        col = lax.rem(tile, 4) * 128
        cols = pl.ds(pl.multiple_of(col, 128), 128)
        cols_im = pl.ds(pl.multiple_of(col + BLK, 128), 128)
        planes = widx[:, lanes]
        offset = (offs[0, :, lanes], offs[1, :, lanes])
        for g in range(GROUPS):
            b = g * 8 + blk
            plane = jnp.broadcast_to(planes[g : g + 1], (8, 128))
            val_re = jnp.take_along_axis(tab_re, plane, axis=1)
            val_im = jnp.take_along_axis(tab_im, plane, axis=1)
            for side in range(2):
                off = jnp.broadcast_to(offset[side][g : g + 1], (8, 128))
                dist = iota8 - off
                cyc = lax.bitwise_and(dist, 7)
                tap_re = jnp.take_along_axis(val_re, cyc, axis=0)
                tap_im = jnp.take_along_axis(val_im, cyc, axis=0)
                res, ims = [], []
                for q in range(SG // 8):
                    ok = lax.bitwise_and(dist + 8 * q, -8) == 0
                    res.append(jnp.where(ok, tap_re, 0.0))
                    ims.append(jnp.where(ok, tap_im, 0.0))
                k_re = jnp.concatenate(res, axis=0)
                k_im = jnp.concatenate(ims, axis=0)
                if side == 0:
                    re16 = k_re.astype(BF)
                    left[b, 0:SG, cols] = re16
                    left[b, 0:SG, cols_im] = (-k_im).astype(BF)
                    left[b, SG : 2 * SG, cols] = k_im.astype(BF)
                    left[b, SG : 2 * SG, cols_im] = re16
                else:
                    right[b, 0, :, cols] = k_re
                    right[b, 1, :, cols] = k_im
        return carry

    lax.fori_loop(0, GROUPS * BLK // 128, prep, 0)

    def grid_part(st, lo, hi, run):
        def body(j, run):
            b = plan[0, j]
            kern = right[b]
            k_re = kern[0]
            k_im = kern[1]
            seen = recv[st][b]
            rows = []
            for c in range(CPS):
                v = seen[c].astype(F32)
                for p in range(POL):
                    v_re = jnp.broadcast_to(v[p : p + 1], (SG, BLK))
                    v_im = jnp.broadcast_to(v[p + POL : p + POL + 1], (SG, BLK))
                    y_re = (v_re * k_re - v_im * k_im).astype(BF)
                    y_im = (v_re * k_im + v_im * k_re).astype(BF)
                    rows.append(jnp.concatenate([y_re, y_im], axis=1))
            y = jnp.concatenate(rows, axis=0)
            o = lax.dot_general(
                left[b], y, (((1,), (1,)), ((), ())), preferred_element_type=F32
            )
            run = run * plan[1, j].astype(F32) + o
            pref[j] = run
            return run

        return lax.fori_loop(lo, hi, body, run, unroll=8)

    def emit(st):
        def body(s, carry):
            part[st, s] = (pref[plan[2, s]] * plan[3, s].astype(F32)).astype(BF)
            return carry

        lax.fori_loop(0, NSUB, body, 0)

    def ring_copy(st, half, phase, k, src, dst, dev):
        return pltpu.make_async_remote_copy(
            src_ref=src,
            dst_ref=dst,
            send_sem=ring_send.at[st, half, phase, k - 1],
            recv_sem=ring_recv.at[st, half, phase, k - 1],
            device_id=dev,
            device_id_type=MESH,
        )

    copies = {}
    half_n = NSUB // 2
    first = (mx, mz)
    second = (mz, mx)

    def dev_of(half, phase_axis, k):
        along_x = (half == 0) == (phase_axis == 0)
        return (x_peer(k), on_x(x_peer(k))) if along_x else (z_peer(k), on_z(z_peer(k)))

    def rs1(st):
        for half in range(2):
            for k in range(1, RING):
                pos, dev = dev_of(half, 0, k)
                cp = ring_copy(
                    st,
                    half,
                    0,
                    k,
                    part.at[st, pl.ds(half * half_n + 4 * pos, 4)],
                    in1.at[st, half, k - 1],
                    dev,
                )
                cp.start()
                copies[st, half, 0, k] = cp

    def rs2(st):
        for half in range(2):
            for k in range(1, RING):
                copies[st, half, 0, k].wait()
            total = part[st, pl.ds(half * half_n + 4 * first[half], 4)].astype(F32)
            for k in range(1, RING):
                total = total + in1[st, half, k - 1].astype(F32)
            mid[st, half] = total.astype(BF)
            for k in range(1, RING):
                pos, dev = dev_of(half, 1, k)
                cp = ring_copy(st, half, 1, k, mid.at[st, half, pos], in2.at[st, half, k - 1], dev)
                cp.start()
                copies[st, half, 1, k] = cp

    def ag1(st):
        for half in range(2):
            for k in range(1, RING):
                copies[st, half, 1, k].wait()
            total = mid[st, half, second[half]].astype(F32)
            for k in range(1, RING):
                total = total + in2[st, half, k - 1].astype(F32)
            slot = half * half_n + 4 * first[half] + second[half]
            grid_out[st, slot] = total.astype(BF)
            for k in range(1, RING):
                pos, dev = dev_of(half, 1, k)
                cp = ring_copy(
                    st, half, 2, k, grid_out.at[st, slot], grid_out.at[st, slot], dev
                )
                cp.start()
                copies[st, half, 2, k] = cp

    def ag2(st):
        for half in range(2):
            for k in range(1, RING):
                copies[st, half, 2, k].wait()
            span = pl.ds(half * half_n + 4 * first[half], 4)
            for k in range(1, RING):
                pos, dev = dev_of(half, 0, k)
                cp = ring_copy(
                    st, half, 3, k, grid_out.at[st, span], grid_out.at[st, span], dev
                )
                cp.start()
                copies[st, half, 3, k] = cp

    def finish(st):
        for half in range(2):
            for k in range(1, RING):
                copies[st, half, 3, k].wait()

    pending = []

    def advance():
        for todo in pending:
            todo.pop(0)()
        pending[:] = [todo for todo in pending if todo]

    for st in range(STAGES):
        turned(st)
        run = jnp.zeros((2 * SG, NL), F32)
        for piece in range(2):
            run = grid_part(st, piece * (NB // 2), (piece + 1) * (NB // 2), run)
            advance()
        emit(st)
        rs1(st)
        pending.append([lambda st=st, f=f: f(st) for f in (rs2, ag1, ag2, finish)])
    while pending:
        advance()


def gridded(vis, w_index, offsets, table, plan):
    any_spec = pl.BlockSpec(memory_space=pl.ANY)
    vmem = pl.BlockSpec(memory_space=pltpu.VMEM)
    smem = pl.BlockSpec(memory_space=pltpu.SMEM)
    return pl.pallas_call(
        gather_kernel,
        out_shape=jax.ShapeDtypeStruct((STAGES, NSUB, 2 * SG, NL), BF),
        in_specs=[any_spec, any_spec, any_spec, vmem, smem],
        out_specs=vmem,
        scratch_shapes=[
            *[pltpu.VMEM((NB, CPS, 2 * POL, BLK), BF)] * STAGES,
            pltpu.VMEM((GROUPS, GROUPS * BLK), jnp.int32),
            pltpu.VMEM((2, GROUPS, GROUPS * BLK), jnp.int32),
            pltpu.VMEM((NB, 2 * SG, 2 * BLK), BF),
            pltpu.VMEM((NB, 2, SG, BLK), F32),
            pltpu.VMEM((NB, 2 * SG, NL), F32),
            pltpu.VMEM((STAGES, NSUB, 2 * SG, NL), BF),
            pltpu.VMEM((STAGES, 2, RING - 1, 4, 2 * SG, NL), BF),
            pltpu.VMEM((STAGES, 2, 4, 2 * SG, NL), BF),
            pltpu.VMEM((STAGES, 2, RING - 1, 2 * SG, NL), BF),
            pltpu.SemaphoreType.DMA((2,)),
            pltpu.SemaphoreType.DMA((STAGES, GROUPS - 1)),
            pltpu.SemaphoreType.DMA((STAGES, GROUPS - 1)),
            pltpu.SemaphoreType.DMA((STAGES,)),
            pltpu.SemaphoreType.DMA((STAGES, 2, 4, RING - 1)),
            pltpu.SemaphoreType.DMA((STAGES, 2, 4, RING - 1)),
        ],
        compiler_params=pltpu.CompilerParams(
            collective_id=0, has_side_effects=True, vmem_limit_bytes=60 * 2**20
        ),
        name="turn_grid_share",
    )(vis, w_index, offsets, table, plan)


XT = 256
NT = FX // XT // 2
KH = NSUB * SG
KQ = 128


def flipped(x):
    lanes = 127 - lax.broadcasted_iota(jnp.int32, x.shape, 1)
    return jnp.take_along_axis(x, lanes, axis=1)


def image_kernel(
    rows_s, count_s, grids, row_tab, base, cells, spin, centre, out,
    z_re, z_im, col_c, col_s, cur, buf, sems,
):
    step = pl.program_id(0)
    slot = lax.rem(step, 2)
    facet = lax.axis_index("facet")
    tall = CH * POL * FY

    def fill(blocks):
        for q in range(KH // KQ):
            rows = pl.ds(q * KQ, KQ)
            turn = pl.ds((q % 2) * KQ, KQ)
            wc = spin[0, turn]
            ws = spin[1, turn]
            c = cur[0, rows]
            s = cur[1, rows]
            for h in range(blocks):
                col_c[rows, pl.ds(h * 128, 128)] = c.astype(BF)
                col_s[rows, pl.ds(h * 128, 128)] = s.astype(BF)
                c, s = c * wc - s * ws, s * wc + c * ws
            cur[0, rows] = c
            cur[1, rows] = s

    def writes(n, at):
        right = FX // 2 + n * XT
        left = FX // 2 - XT - n * XT
        return [
            pltpu.make_async_copy(
                buf.at[at, side],
                out.at[:, :, :, pl.ds(pl.multiple_of(lo, XT), XT)],
                sems.at[at, side],
            )
            for side, lo in ((0, right), (1, left))
        ]

    @pl.when(step == 0)
    def _():
        img_scale = 1.0 / math.sqrt(GROUPS * 65536)

        def rows4(q, carry):
            tc = centre[0, facet, q]
            ts = centre[1, facet, q]
            lanes = pl.ds(pl.multiple_of(q * 128, 128), 128)
            for st in range(STAGES):
                os = []
                for gi in range(4):
                    g = q * 4 + gi
                    os.append(jnp.dot(row_tab[g], grids[st, g], preferred_element_type=F32))
                for c in range(CPS):
                    for p in range(POL):
                        lo = c * POL * SG + p * SG
                        both = jnp.concatenate([o[:, lo : lo + SG] for o in os], axis=1)
                        both = both * img_scale
                        re, im = both[:FY], both[FY:]
                        at = (st * CPS + c) * POL * FY + p * FY
                        z_re[pl.ds(at, FY), lanes] = (re * tc - im * ts).astype(BF)
                        z_im[pl.ds(at, FY), lanes] = (re * ts + im * tc).astype(BF)
            return carry

        lax.fori_loop(0, NSUB // 4, rows4, 0)
        for g in range(NSUB):
            rows = pl.ds(g * SG, SG)
            c = base[0, g : g + 1]
            s = base[1, g : g + 1]
            cur[0, rows] = cells[0] * c - cells[1] * s
            cur[1, rows] = cells[1] * c + cells[0] * s

    fill(XT // 128)
    even = jnp.dot(z_re[...], col_c[...], preferred_element_type=F32)
    odd = jnp.dot(z_im[...], col_s[...], preferred_element_type=F32)

    @pl.when(step >= 2)
    def _():
        for cp in writes(step - 2, slot):
            cp.wait()

    buf[slot, 0] = (even - odd).reshape(CH, POL, FY, XT)
    both = even + odd
    buf[slot, 1, :, :, :, 0:128] = flipped(both[:, 128:]).reshape(CH, POL, FY, 128)
    buf[slot, 1, :, :, :, 128:] = flipped(both[:, :128]).reshape(CH, POL, FY, 128)

    @pl.when(step == NT - 1)
    def _():
        fill(1)
        before = jnp.maximum(facet - 1, 0)
        lines = lax.broadcasted_iota(jnp.int32, (FY, MARGIN), 0)
        used = jnp.where(facet > 0, count_s[before], 0)
        keep = jnp.zeros((FY, MARGIN), F32)
        for i in range(32):
            row = jnp.where(i < used, rows_s[before, i], -1)
            keep = keep + jnp.where(lines == row, 1.0, 0.0)
        edge = jnp.dot(z_re[...], col_c[:, 0:MARGIN], preferred_element_type=F32) + jnp.dot(
            z_im[...], col_s[:, 0:MARGIN], preferred_element_type=F32
        )
        edge = flipped(edge).reshape(CH, POL, FY, MARGIN) * keep
        buf[slot, 1, :, :, :, 0:MARGIN] = buf[slot, 1, :, :, :, 0:MARGIN] + edge

    for cp in writes(step, slot):
        cp.start()

    @pl.when(step == NT - 1)
    def _():
        for cp in writes(step - 1, 1 - slot) + writes(step, slot):
            cp.wait()


def imaged(grids, rows_list, counts, *tables):
    def whole(shape):
        return pl.BlockSpec(shape, lambda n: (0,) * len(shape), pipeline_mode=pl.Buffered(1))

    smem = pl.BlockSpec(memory_space=pltpu.SMEM)
    return pl.pallas_call(
        image_kernel,
        grid=(NT,),
        out_shape=jax.ShapeDtypeStruct((CH, POL, FY, FX), F32),
        in_specs=[smem, smem] + [whole(a.shape) for a in (grids, *tables)],
        out_specs=pl.BlockSpec(memory_space=pl.ANY),
        scratch_shapes=[
            pltpu.VMEM((CH * POL * FY, KH), BF),
            pltpu.VMEM((CH * POL * FY, KH), BF),
            pltpu.VMEM((KH, XT), BF),
            pltpu.VMEM((KH, XT), BF),
            pltpu.VMEM((2, KH, 128), F32),
            pltpu.VMEM((2, 2, CH, POL, FY, XT), F32),
            pltpu.SemaphoreType.DMA((2, 2)),
        ],
        compiler_params=pltpu.CompilerParams(vmem_limit_bytes=60 * 2**20),
        name="facet_image",
    )(rows_list, counts, grids, *tables)


def waves(turns, period):
    rad = np.mod(turns, period).astype(np.float64) * (2.0 * math.pi / period)
    return jnp.asarray(np.stack([np.cos(rad), np.sin(rad)]), F32)


def row_table():
    g = np.arange(NSUB)
    span = NX // SG
    anchor = ((37 * g) % span - span // 2) * SG
    lines = np.arange(FY) - FY // 2
    phase = ((anchor[:, None, None] + np.arange(SG)[None, None, :]) * lines[None, :, None]) % NX
    rad = phase.astype(np.float32) * np.float32(2.0 * math.pi / NX)
    cos, sin = np.cos(rad), np.sin(rad)
    top = np.concatenate([cos, -sin], axis=2)
    low = np.concatenate([sin, cos], axis=2)
    return np.concatenate([top, low], axis=1)


def shards(
    visibilities, w_kernel, w_index, cell_offsets, block_sub, intersection_rows, intersection_count
):
    vis = visibilities.reshape(visibilities.shape[0], 2 * POL, w_index.shape[1])
    table = w_kernel.transpose(1, 2, 0)
    grids = gridded(vis, w_index, cell_offsets, table, sort_plan(block_sub))

    g = np.arange(NSUB)
    span = NX // SG
    anchor = ((53 * g + 5) % span - span // 2) * SG
    freq = (anchor[:, None] + np.arange(SG)[None, :]).reshape(-1, 1)
    twice = 2 * np.arange(128)[None, :] + 1
    ones = np.ones((1, 128), np.int64)
    base = waves(anchor[:, None] * twice, 2 * NX)
    cells = waves(np.arange(SG)[:, None] * twice, 2 * NX)
    spin = waves(freq[: 2 * KQ] * 128 * ones, NX)
    middle = 2 * (np.arange(NX // FX) * FX - NX // 2) + FX - 1
    centre = waves(middle[:, None, None, None] * freq.reshape(1, KH // 128, 1, 128), 2 * NX)
    assert np.all((freq.reshape(-1, 2 * KQ) * 128 - freq[: 2 * KQ].T * 128) % NX == 0)

    return imaged(
        grids,
        intersection_rows,
        intersection_count,
        jnp.asarray(row_table(), BF),
        base,
        cells,
        spin,
        centre,
    )


def solution(mesh):
    return jax.shard_map(
        shards,
        mesh=mesh,
        in_specs=(
            P(None, None, "chan", "facet"),
            P(),
            P(None, "facet"),
            P(None, None, "facet"),
            P(None, "facet"),
            P(),
            P(),
        ),
        out_specs=P("chan", None, None, "facet"),
        check_vma=False,
    )
```
